32 devices in a mesh: blk: 8 (over z, x), rep: 4 (over y, core).
Axes of the slice: x: 2, y: 2, z: 4, core: 2. Of those that a mesh axis runs over, the one named last changes fastest.
Arguments:
- amplitudes: bfloat16 [256, 24576], P(None, ('blk', 'rep')), may hold values from -6 to 6
- panels: bfloat16 [1376, 192, 768], P(('blk', 'rep')), may hold values from -0.21875 to 0.21875
- panel_owner_index: int32 [1376, 1], P(('blk', 'rep')), may hold values from 0 to 7; in each aligned block of 43 rows (0 to 42, 43 to 85, ...) at most 11 rows name the same one
- panel_target_tile: int32 [1376], P(('blk', 'rep')), may hold values from 0 to 15
- panel_tile_mask: int32 [1376, 4], P(('blk', 'rep')), may hold values 0 or 1
- tile_sizes: int32 [128], replicated, may hold values from 64 to 192
- tile_irreps: int32 [128], replicated, may hold values from 0 to 1
- occ_energy: float32 [256], P('rep'), may hold values from -3 to -0.5
- vir_energy: float32 [24576], P('blk'), may hold values from 0.5 to 6
Outputs:
- doubles_update: bfloat16 [256, 24576], P('rep', 'blk')
The draws below stay inside these ranges and needn't reach their ends.
Inputs may be any that keep to these rules, and one draw needn't show every extreme that they name: `panel_owner_index`: within the 43 rows of one device no index of blk is named more than 11 times, a bound that some block reaches.
All inputs are finite; a program needn't handle non-finite values. No bound on the sum of `panel_tile_mask` on one device may be relied on, other than what follows from the above.
Results may differ from the reference program's by a relative error of at most 0.0049.
Values may be sent and summed in bfloat16 or wider, within the bound.
No kernel may reach another device: no remote copies, remote signals or barrier semaphores. Data moves between devices by JAX's collectives and lax.ppermute only.
A program may use at most 128 MiB of HBM per device.

```python
import math
import jax
import jax.numpy as jnp
import numpy as np
from jax import lax

TILE_SLOTS = 192
AMP_TILE_COUNT = 4
DEVICE_PANELS = 43
IRREPS = 2
ROWS = 256
RESULT_TILES = 16
NT = 128
TOTAL_PANELS = 1376
PANEL_LIMIT = 11
N_BLK = 8
DEVICES = 32


def draw_tile_sizes(key, part):
    first_key, second_key, third_key = jax.random.split(jax.random.fold_in(key, 7), 3)
    sizes_drawn = jax.random.randint(first_key, (NT,), TILE_SLOTS // 3, TILE_SLOTS + 1)
    top_place = jax.random.randint(second_key, (), 0, NT)
    low_place = (top_place + 1 + jax.random.randint(third_key, (), 0, NT - 1)) % NT
    sizes_drawn = sizes_drawn.at[top_place].set(TILE_SLOTS).at[low_place].set(TILE_SLOTS // 3)
    return sizes_drawn.astype(jnp.int32)


def touch_ends(values, own_key, least, high):
    extent = values.shape
    place = [jax.random.randint(jax.random.fold_in(own_key, axis), (), 0, extent[axis]) for axis in range(len(extent))]
    values = values.at[tuple(place)].set(least)
    longest = extent.index(max(extent))
    place[longest] = (place[longest] + 1) % extent[longest]
    return values.at[tuple(place)].set(high)


def block_scale(rng, extent, cuts, least, top_value):
    loudness, own = 1.0, jax.random.fold_in(rng, 6)
    for position, shards_of in cuts:
        draws = jnp.exp(jax.random.uniform(jax.random.fold_in(own, position), (shards_of,), jnp.float32, least / len(cuts), top_value / len(cuts)))
        loudness = loudness * jnp.repeat(draws, extent[position] // shards_of).reshape([-1 if axis == position else 1 for axis in range(len(extent))])
    return loudness


def routed_block(key, own, number, rows, amount, top, limit, slope):
    order = jax.random.permutation(key, amount)
    heavy_load, usual = portions_of(amount, rows * top, limit, slope, True), portions_of(amount, rows * top, limit, slope, False)
    places = jnp.arange(amount)

    def named(sizes, rotation):
        used = int((sizes > 0).sum())
        fixed = max(1, used // 4)
        passed = fixed + (places - fixed + rotation * (used - fixed)) % max(1, amount - fixed)
        return jnp.zeros((amount,), jnp.int32).at[order[jnp.where(places < fixed, places, passed)]].set(jnp.asarray(sizes, jnp.int32))

    sizes = jnp.where(number % 4 == 0, named(heavy_load, number // 4), named(usual, number - number // 4 - 1))
    mixed = jax.random.permutation(jax.random.fold_in(own, 3), amount)
    source_of, sink = mixed[0:amount // 2 * 2:2], mixed[1:amount // 2 * 2:2]
    margin = jnp.minimum(sizes[source_of] - 1, limit - sizes[sink]) // 2
    margin = jnp.where((source_of == order[0]) | (sink == order[0]) | (sizes[sink] == 0), 0, jnp.maximum(margin, 0))
    passed = jax.random.randint(jax.random.fold_in(own, 4), (amount // 2,), 0, 1 << 20) % (margin + 1)
    sizes = sizes.at[source_of].add(-passed).at[sink].add(passed)
    items = jnp.searchsorted(jnp.cumsum(sizes), jnp.arange(rows * top), side="right").astype(jnp.int32)
    grid = items.reshape(top, rows).T
    grid = grid[jax.random.permutation(jax.random.fold_in(own, 1), rows)]
    rotation = jax.random.randint(jax.random.fold_in(own, 2), (rows, 1), 0, top)
    return jnp.take_along_axis(grid, (jnp.arange(top)[None, :] + rotation) % top, axis=1)


def portions_of(number_of, total, bound, lean, full):
    loads = [(1 << 20) // math.isqrt(standing ** lean) + 1 for standing in range(1, number_of + 1)]
    largest = bound if full else min(bound, max(-(-total // number_of), total * loads[0] // sum(loads)))
    least = 1 if total - largest >= number_of - 1 else 0
    given, surplus = [largest] + [least] * (number_of - 1), total - largest - least * (number_of - 1)
    while surplus > 0:
        free = [i for i in range(1, number_of) if given[i] < largest] or [i for i in range(1, number_of) if given[i] < bound]
        whole, budget = sum([loads[i] for i in free]), surplus
        for i in free:
            more = min(bound - given[i], max(1, budget * loads[i] // whole), surplus)
            given[i] = given[i] + more
            surplus = surplus - more
    return np.array(given)


def gaussian(key, dims, scale, reach, cuts=(), kind=jnp.bfloat16):
    gain = block_scale(key, dims, cuts, -0.22, 0.18) if cuts else 1.0
    drawn = jax.random.normal(key, dims, jnp.float32) * scale * gain
    return jnp.minimum(jnp.maximum(drawn, -reach), reach).astype(kind)


def setup_inputs(seed: int = 0) -> dict:
    streams_of = jax.random.split(jax.random.key(seed), 10)
    amplitudes = gaussian(streams_of[0], (ROWS, NT * TILE_SLOTS), 1.0, 6.0, ((1, 32),))
    panels = gaussian(streams_of[1], (TOTAL_PANELS, TILE_SLOTS, AMP_TILE_COUNT * TILE_SLOTS), (AMP_TILE_COUNT * TILE_SLOTS) ** -0.5, 0.21875, ((0, 32),))
    panel_owner_index_keys = jax.random.split(jax.random.fold_in(streams_of[2], 1), TOTAL_PANELS // DEVICE_PANELS)
    panel_owner_index_turns = jax.random.permutation(jax.random.fold_in(streams_of[2], 3), TOTAL_PANELS // DEVICE_PANELS)
    panel_owner_index = jax.vmap(lambda own, number: routed_block(jax.random.fold_in(streams_of[2], 2), own, number, DEVICE_PANELS, N_BLK, 1, PANEL_LIMIT, 2))(panel_owner_index_keys, panel_owner_index_turns).reshape((TOTAL_PANELS, 1))
    panel_target_tile = touch_ends(jax.random.randint(streams_of[3], (TOTAL_PANELS,), 0, RESULT_TILES), jax.random.fold_in(streams_of[3], 1), 0, RESULT_TILES - 1).astype(jnp.int32)
    panel_tile_mask = touch_ends((jax.random.randint(streams_of[4], (TOTAL_PANELS, AMP_TILE_COUNT), 0, 3) < 2).astype(jnp.int32), jax.random.fold_in(streams_of[4], 1), 0, 1)
    tile_sizes = draw_tile_sizes(jax.random.fold_in(streams_of[9], 71), 0)
    tile_irreps = touch_ends(jax.random.randint(streams_of[6], (NT,), 0, IRREPS), jax.random.fold_in(streams_of[6], 1), 0, IRREPS - 1).astype(jnp.int32)
    occ_energy = jnp.clip(-3.0 + 2.5 * jax.random.uniform(streams_of[7], (ROWS,), jnp.float32) ** block_scale(streams_of[7], (ROWS,), ((0, 4),), -0.2, 0.2), -3.0, -0.5)
    vir_energy = jnp.clip(0.5 + 5.5 * jax.random.uniform(streams_of[8], (NT * TILE_SLOTS,), jnp.float32) ** block_scale(streams_of[8], (NT * TILE_SLOTS,), ((0, 8),), -0.2, 0.2), 0.5, 6.0)
    return {"amplitudes": amplitudes, "panels": panels, "panel_owner_index": panel_owner_index, "panel_target_tile": panel_target_tile, "panel_tile_mask": panel_tile_mask, "tile_sizes": tile_sizes, "tile_irreps": tile_irreps, "occ_energy": occ_energy, "vir_energy": vir_energy}


def reference(amplitudes, panels, panel_owner_index, panel_target_tile, panel_tile_mask, tile_sizes, tile_irreps, occ_energy, vir_energy):
    in_tile = jnp.arange(TILE_SLOTS, dtype=jnp.int32)
    owner_list = panel_owner_index[:, 0]

    def one_device(ladder, device):
        first_col = (device * (AMP_TILE_COUNT * TILE_SLOTS)).astype(jnp.int32)
        columns = lax.dynamic_slice_in_dim(amplitudes, first_col, AMP_TILE_COUNT * TILE_SLOTS, 1)
        sizes_here = lax.dynamic_slice_in_dim(tile_sizes, (device * AMP_TILE_COUNT).astype(jnp.int32), AMP_TILE_COUNT, 0)
        keep_cols = (in_tile[None, :] < sizes_here[:, None]).reshape(AMP_TILE_COUNT * TILE_SLOTS)
        columns = jnp.where(keep_cols[None, :], columns, jnp.zeros_like(columns))
        first_slot = (device * DEVICE_PANELS).astype(jnp.int32)
        panel_block = lax.dynamic_slice_in_dim(panels, first_slot, DEVICE_PANELS, 0)
        owners = lax.dynamic_slice_in_dim(owner_list, first_slot, DEVICE_PANELS, 0)
        targets = lax.dynamic_slice_in_dim(panel_target_tile, first_slot, DEVICE_PANELS, 0)
        masks = lax.dynamic_slice_in_dim(panel_tile_mask, first_slot, DEVICE_PANELS, 0)
        tile_target = (owners * RESULT_TILES + targets).astype(jnp.int32)
        irrep_source = lax.dynamic_slice_in_dim(tile_irreps, (device * AMP_TILE_COUNT).astype(jnp.int32), AMP_TILE_COUNT, 0)
        irrep_target = tile_irreps[tile_target]
        live_blocks = masks * (irrep_source[None, :] == irrep_target[:, None]).astype(jnp.int32)
        scaled = panel_block.astype(jnp.float32).reshape(DEVICE_PANELS, TILE_SLOTS, AMP_TILE_COUNT, TILE_SLOTS) * live_blocks.astype(jnp.float32)[:, None, :, None]
        partial_value = jnp.einsum("slk,rk->slr", scaled.reshape(DEVICE_PANELS, TILE_SLOTS, AMP_TILE_COUNT * TILE_SLOTS), columns.astype(jnp.float32), precision=lax.Precision.HIGHEST).astype(jnp.bfloat16)
        ladder = ladder.at[tile_target].add(partial_value.astype(jnp.float32))
        return ladder, None

    start = jnp.zeros((NT, TILE_SLOTS, ROWS), jnp.float32)
    ladder, unused = lax.scan(one_device, start, jnp.arange(DEVICES, dtype=jnp.int32))
    ladder_rows = ladder.reshape(NT * TILE_SLOTS, ROWS).T
    keep_out = (in_tile[None, :] < tile_sizes[:, None]).reshape(NT * TILE_SLOTS)
    denominator = occ_energy[:, None] - vir_energy[None, :]
    result = jnp.where(keep_out[None, :], ladder_rows / denominator, jnp.zeros_like(ladder_rows))
    return result.astype(jnp.bfloat16)
```

```python
import functools

import jax
import jax.numpy as jnp
from jax import lax
from jax.experimental import pallas as pl
from jax.experimental.pallas import tpu as pltpu
from jax.sharding import PartitionSpec as P

LANES = 128
PANEL_BLOCK = 11
PARTS = (32, 32, 16, 16)


def stage_factors(count):
    factors, rest = [], count
    while rest > 1:
        factor = min(4 if factors else 2, rest)
        factors.append(factor)
        rest //= factor
    return factors


def whole(memory_space=pltpu.VMEM):
    return pl.BlockSpec(memory_space=memory_space)


def half_rows(low, high):
    lane = lax.broadcasted_iota(jnp.int32, low.shape, low.ndim - 1)
    width = LANES // 2
    first = jnp.where(lane < width, low, pltpu.roll(high, width, high.ndim - 1))
    second = jnp.where(lane < width, pltpu.roll(low, width, low.ndim - 1), high)
    return first, second


def partial_kernel(place, target, mask, sizes, irreps, amp, panels, *refs):
    outs, amp_t, masked = refs[:-2], refs[-2], refs[-1]
    rep_count, row_count, depth = amp.shape
    block, halves, rows, _ = panels.shape
    count = target.shape[0]
    tiles = mask.shape[0] // count
    width = depth // tiles
    device, rep_index = place[0], place[1]
    step = pl.program_id(0)

    @pl.when(step == 0)
    def _():
        ordered = jnp.concatenate([amp[rep_index ^ k] for k in range(rep_count)], axis=0)
        amp_t[...] = ordered.T

    column = lax.broadcasted_iota(jnp.int32, (1, depth), 1)
    for p in range(block):
        s = jnp.minimum(step * block + p, count - 1)
        irrep_target = irreps[target[s]]
        keep = None
        for j in range(tiles):
            source = device * tiles + j
            live = (mask[s * tiles + j] != 0) & (irreps[source] == irrep_target)
            limit = jnp.where(live, sizes[source], 0)
            inside = (column >= j * width) & (column < j * width + limit)
            keep = inside if keep is None else keep | inside
        factor = keep.astype(jnp.float32).astype(jnp.bfloat16)
        for h in range(halves):
            masked[pl.ds((p * halves + h) * rows, rows), :] = panels[p, h] * factor
    product = jnp.dot(masked[...], amp_t[...], preferred_element_type=jnp.float32)
    product = product.reshape(block, halves, rows, rep_count * row_count)
    for pair in range(rep_count // 2):
        lanes = slice(pair * LANES, (pair + 1) * LANES)
        first, second = half_rows(product[:, 0, :, lanes], product[:, 1, :, lanes])
        outs[2 * pair][...] = first.astype(jnp.bfloat16)
        outs[2 * pair + 1][...] = second.astype(jnp.bfloat16)


def partials(place, target, mask, sizes, irreps, amp, panels, first, rows):
    count, halves, _, depth = panels.shape
    rep_count, row_count, _ = amp.shape
    part = first // rows
    out = jax.ShapeDtypeStruct((count, rows, LANES), jnp.bfloat16)
    return pl.pallas_call(
        partial_kernel,
        out_shape=[out] * rep_count,
        grid_spec=pltpu.PrefetchScalarGridSpec(
            num_scalar_prefetch=5,
            grid=(pl.cdiv(count, PANEL_BLOCK),),
            in_specs=[
                pl.BlockSpec(amp.shape, lambda i, *_: (0, 0, 0)),
                pl.BlockSpec((PANEL_BLOCK, halves, rows, depth), lambda i, *_: (i, 0, part, 0)),
            ],
            out_specs=[pl.BlockSpec((PANEL_BLOCK, rows, LANES), lambda i, *_: (i, 0, 0))] * rep_count,
            scratch_shapes=[
                pltpu.VMEM((depth, rep_count * row_count), jnp.bfloat16),
                pltpu.VMEM((PANEL_BLOCK * halves * rows, depth), jnp.bfloat16),
            ],
        ),
        cost_estimate=pl.CostEstimate(
            flops=2 * count * halves * rows * depth * rep_count * row_count,
            bytes_accessed=2 * count * halves * rows * (depth + rep_count * row_count),
            transcendentals=0,
        ),
        name="partials",
    )(place, target, mask, sizes, irreps, amp, panels)


def gather_kernel(factor, place, *refs):
    ids = refs[: (len(refs) - 1 - factor) // 2]
    parts = refs[len(ids) : 2 * len(ids)]
    outs, ladder = refs[2 * len(ids) : -1], refs[-1]
    count = ids[0].shape[0]
    rest, tiles = outs[0].shape[:2]
    ladder[...] = jnp.zeros_like(ladder)

    def add(s, carry):
        for index, part in zip(ids, parts):
            ladder[index[s]] += part[s].astype(jnp.float32)
        return carry

    lax.fori_loop(0, count, add, 0)
    digit = place[2]
    for k in range(factor):
        for z in range(rest):
            tile = (z * factor + (digit ^ k)) * tiles
            outs[k][z] = ladder[pl.ds(tile, tiles)].astype(outs[k].dtype)


def gather_tiles(place, ids, parts, blk_count, tiles, factor):
    rows = parts[0].shape[1]
    rest = blk_count // factor
    shape = (rest, tiles, rows, LANES)
    outs = [jax.ShapeDtypeStruct(shape, jnp.bfloat16 if k else jnp.float32) for k in range(factor)]
    return pl.pallas_call(
        functools.partial(gather_kernel, factor),
        out_shape=outs,
        in_specs=[whole(pltpu.SMEM)] * (1 + len(ids)) + [whole()] * len(parts),
        out_specs=[whole()] * factor,
        scratch_shapes=[pltpu.VMEM((blk_count * tiles, rows, LANES), jnp.float32)],
        compiler_params=pltpu.CompilerParams(vmem_limit_bytes=60 << 20),
        cost_estimate=pl.CostEstimate(
            flops=blk_count * tiles * rows * LANES,
            bytes_accessed=8 * blk_count * tiles * rows * LANES,
            transcendentals=0,
        ),
        name="gather_tiles",
    )(place, *ids, *parts)


def merge_kernel(factor, position, place, *refs):
    ins, outs = refs[:-factor], refs[-factor:]
    rest = outs[0].shape[0]
    digit = place[position]
    for k in range(factor):
        for z in range(rest):
            owner = z * factor + (digit ^ k)
            total = ins[0][owner]
            for other in ins[1:]:
                total = total + other[owner].astype(jnp.float32)
            outs[k][z] = total.astype(outs[k].dtype)


def merge(place, position, arrays, factor):
    owners, tiles, rows, _ = arrays[0].shape
    shape = (owners // factor, tiles, rows, LANES)
    outs = [jax.ShapeDtypeStruct(shape, jnp.bfloat16 if k else jnp.float32) for k in range(factor)]
    return pl.pallas_call(
        functools.partial(merge_kernel, factor, position),
        out_shape=outs,
        in_specs=[whole(pltpu.SMEM)] + [whole()] * len(arrays),
        out_specs=[whole()] * factor,
        compiler_params=pltpu.CompilerParams(vmem_limit_bytes=60 << 20),
        cost_estimate=pl.CostEstimate(
            flops=owners * tiles * rows * LANES,
            bytes_accessed=8 * owners * tiles * rows * LANES,
            transcendentals=0,
        ),
        name="merge",
    )(place, *arrays)


def finish_kernel(per_part, *refs):
    occ, vir, keep, out = refs[0], refs[1], refs[2], refs[-1]
    ins = refs[3:-1]
    tiles = ins[0].shape[0]
    totals = []
    for start in range(0, len(ins), per_part):
        total = ins[start][...]
        for other in ins[start + 1 : start + per_part]:
            total = total + other[...].astype(jnp.float32)
        totals.append(total)
    total = jnp.concatenate(totals, axis=1)
    half = tiles // 2
    first, second = half_rows(total[:half], total[half:])
    rows = jnp.stack([first, second], axis=1).reshape(-1, LANES)
    flipped = rows.T
    columns = rows.shape[0]
    row_count = out.shape[0]
    for side in range(2):
        lanes = slice(side * columns, (side + 1) * columns)
        value = flipped[side * row_count : (side + 1) * row_count]
        denominator = occ[...] - vir[:, lanes]
        kept = keep[:, lanes] != 0
        out[:, lanes] = jnp.where(kept, value / denominator, 0.0).astype(jnp.bfloat16)


def finish(occ, vir, keep, arrays, per_part):
    return pl.pallas_call(
        functools.partial(finish_kernel, per_part),
        out_shape=jax.ShapeDtypeStruct((occ.shape[0], vir.shape[1]), jnp.bfloat16),
        in_specs=[whole()] * (3 + len(arrays)),
        out_specs=whole(),
        compiler_params=pltpu.CompilerParams(vmem_limit_bytes=60 << 20),
        name="finish",
    )(occ, vir, keep, *arrays)


def shards(
    amplitudes,
    panels,
    panel_owner_index,
    panel_target_tile,
    panel_tile_mask,
    tile_sizes,
    tile_irreps,
    occ_energy,
    vir_energy,
):
    blk_count = lax.axis_size("blk")
    rep_count = lax.axis_size("rep")
    blk_index = lax.axis_index("blk")
    rep_index = lax.axis_index("rep")
    count, width, depth = panels.shape
    tiles_here = depth // width
    owned = tiles_here * rep_count
    row_count = amplitudes.shape[0] // rep_count
    halves = LANES // row_count
    packed = width // halves
    factors = stage_factors(blk_count)

    digits, strides, rest, stride = [], [], blk_index, 1
    for factor in factors:
        digits.append(rest % factor)
        strides.append(stride)
        rest, stride = rest // factor, stride * factor
    place = jnp.stack([blk_index * rep_count + rep_index, rep_index, *digits]).astype(jnp.int32)

    target = panel_owner_index[:, 0] * owned + panel_target_tile
    mask = panel_tile_mask.reshape(-1)
    amp = amplitudes.reshape(rep_count, row_count, depth)
    panels = panels.reshape(count, halves, packed, depth)

    def swap_rep(value, k):
        return lax.ppermute(value, "rep", [(i, i ^ k) for i in range(rep_count)])

    def swap_blk(value, k):
        return lax.ppermute(value, "blk", [(i, i ^ k) for i in range(blk_count)])

    ids = [target] + [swap_rep(target, k) for k in range(1, rep_count)]
    collected, first = [], 0
    for rows in PARTS:
        own, *others = partials(
            place, target, mask, tile_sizes, tile_irreps, amp, panels, first, rows
        )
        first += rows
        received = {k: swap_rep(others[k - 1], k) for k in reversed(range(1, rep_count))}
        arrays = gather_tiles(
            place,
            ids,
            [own] + [received[k] for k in range(1, rep_count)],
            blk_count,
            owned,
            factors[0],
        )
        for position, factor in enumerate(factors):
            stride = strides[position]
            arrays = [arrays[0]] + [swap_blk(arrays[k], k * stride) for k in range(1, factor)]
            if position + 1 < len(factors):
                arrays = merge(place, 3 + position, arrays, factors[position + 1])
        collected += [value[0] for value in arrays]

    sizes_owned = lax.dynamic_slice_in_dim(tile_sizes, blk_index * owned, owned, 0)
    in_tile = jnp.arange(width, dtype=jnp.int32)
    keep = (in_tile[None, :] < sizes_owned[:, None]).astype(jnp.int32).reshape(1, owned * width)
    return finish(
        occ_energy[:, None], vir_energy[None, :], keep, collected, len(collected) // len(PARTS)
    )


def solution(mesh):
    return jax.shard_map(
        shards,
        mesh=mesh,
        in_specs=(
            P(None, ("blk", "rep")),
            P(("blk", "rep"), None, None),
            P(("blk", "rep"), None),
            P(("blk", "rep")),
            P(("blk", "rep"), None),
            P(),
            P(),
            P("rep"),
            P("blk"),
        ),
        out_specs=P("rep", "blk"),
        check_vma=False,
    )
```

```python
import functools

import jax
import jax.numpy as jnp
from jax import lax
from jax.experimental import pallas as pl
from jax.experimental.pallas import tpu as pltpu
from jax.sharding import PartitionSpec as P

LANES = 128
COPY_PANELS = 11
SHARES = (4, 3, 3, 2)


def stage_factors(count):
    factors, rest = [], count
    while rest > 1:
        factor = min(4 if factors else 2, rest)
        factors.append(factor)
        rest //= factor
    return factors


def task_order(parts, stages):
    keys = [(part - 2.6, part, -1) for part in range(parts)]
    keys += [(part + 1.5 * stage, part, stage) for part in range(parts) for stage in range(stages)]
    return [(part, stage) for _, part, stage in sorted(keys)]


def whole(memory_space=pltpu.VMEM):
    return pl.BlockSpec(memory_space=memory_space)


def nbytes(*arrays):
    total = 0
    for a in arrays:
        size = jnp.dtype(a.dtype).itemsize
        for d in a.shape:
            size *= d
        total += size
    return total


def grant(*arrays):
    return pltpu.CompilerParams(vmem_limit_bytes=min(62 << 20, nbytes(*arrays) * 3 // 2 + (4 << 20)))


def half_rows(low, high):
    lane = lax.broadcasted_iota(jnp.int32, low.shape, low.ndim - 1)
    width = LANES // 2
    first = jnp.where(lane < width, low, pltpu.roll(high, width, high.ndim - 1))
    second = jnp.where(lane < width, pltpu.roll(low, width, low.ndim - 1), high)
    return first, second


def column_sum(pick, values):
    return jnp.sum(jnp.where(pick, values, 0.0), axis=1, keepdims=True)


def live_factors(owner, tile, mask, sizes, irreps, device, owned, depth):
    tiles, count = mask.shape
    width, total = depth // tiles, sizes.shape[-1]
    eye = lax.broadcasted_iota(jnp.int32, (count, count), 0) == lax.broadcasted_iota(
        jnp.int32, (count, count), 1
    )
    size_row = sizes.reshape(1, total).astype(jnp.float32)
    irrep_row = irreps.reshape(1, total).astype(jnp.float32)
    target_row = owner * owned + tile.reshape(1, count)
    target = column_sum(eye, target_row.astype(jnp.float32)).astype(jnp.int32)
    tile_index = lax.broadcasted_iota(jnp.int32, (count, total), 1)
    irrep_target = column_sum(tile_index == target, irrep_row)
    column = lax.broadcasted_iota(jnp.int32, (count, depth), 1)
    keep = None
    for j in range(tiles):
        source = tile_index[:1] == device * tiles + j
        masked = column_sum(eye, mask[j : j + 1, :].astype(jnp.float32))
        live = (masked != 0.0) & (irrep_target == column_sum(source, irrep_row))
        limit = jnp.where(live, column_sum(source, size_row), 0.0).astype(jnp.int32)
        inside = (column >= j * width) & (column < j * width + limit)
        keep = inside if keep is None else keep | inside
    return target_row, keep.astype(jnp.float32)


def partial_kernel(span, owned, tables, extra, *refs):
    amp, panels = refs[tables : tables + 2]
    outs = refs[tables + 2 + extra :]
    copied, (buffer, amp_here, sem, small) = outs[-4 - tables : -4], outs[-4:]
    rep_count, row_count, depth = amp.shape
    count = panels.shape[0]
    loads = [
        pltpu.make_async_copy(source, target, small.at[i])
        for i, (source, target) in enumerate(zip((*refs[:tables], amp), (*copied, amp_here)))
    ]
    for load in loads:
        load.start()
    first, rows = span
    copies = []
    for start in range(0, count, COPY_PANELS):
        piece = pl.ds(start, min(COPY_PANELS, count - start))
        copies.append(
            pltpu.make_async_copy(
                panels.at[piece, :, pl.ds(first, rows)], buffer.at[piece], sem.at[len(copies)]
            )
        )
        copies[-1].start()
    for load in loads:
        load.wait()

    rep_index = lax.axis_index("rep")
    amp_t = jnp.concatenate([amp_here[rep_index ^ k] for k in range(rep_count)], axis=0).T
    if tables > 1:
        device = lax.axis_index("blk") * rep_count + rep_index
        ids, factors, *outs = outs
        ids[...], factors[...] = live_factors(*[t[...] for t in copied], device, owned, depth)
    else:
        factors = copied[0]

    for copy in copies:
        copy.wait()
    halves = buffer.shape[1]
    factor = factors[...].astype(jnp.bfloat16)
    live_panels = buffer[...] * factor[:, None, None, :]
    product = jnp.dot(
        live_panels.reshape(count * halves * rows, depth),
        amp_t,
        preferred_element_type=jnp.float32,
    )
    product = product.reshape(count, halves, rows, rep_count * row_count)
    for pair in range(rep_count // 2):
        lanes = slice(pair * LANES, (pair + 1) * LANES)
        packed = half_rows(product[:, 0, :, lanes], product[:, 1, :, lanes])
        for side, value in enumerate(packed):
            outs[2 * pair + side][...] = value.astype(jnp.bfloat16)


def partials(tables, amp, panels, span, owned, after=None):
    count, halves, _, depth = panels.shape
    rep_count, row_count, _ = amp.shape
    rows = span[1]
    outs = []
    if len(tables) > 1:
        outs += [
            jax.ShapeDtypeStruct((1, count), jnp.int32),
            jax.ShapeDtypeStruct((count, depth), jnp.float32),
        ]
    heads = len(outs)
    outs += [jax.ShapeDtypeStruct((count, rows, LANES), jnp.bfloat16)] * rep_count
    extra = [] if after is None else [after]
    results = pl.pallas_call(
        functools.partial(partial_kernel, span, owned, len(tables), len(extra)),
        out_shape=outs,
        in_specs=[whole(pl.ANY)] * (len(tables) + 2 + len(extra)),
        out_specs=[whole()] * len(outs),
        scratch_shapes=[
            *[pltpu.VMEM(t.shape, t.dtype) for t in tables],
            pltpu.VMEM((count, halves, rows, depth), jnp.bfloat16),
            pltpu.VMEM(amp.shape, amp.dtype),
            pltpu.SemaphoreType.DMA((pl.cdiv(count, COPY_PANELS),)),
            pltpu.SemaphoreType.DMA((len(tables) + 1,)),
        ],
        compiler_params=pltpu.CompilerParams(
            vmem_limit_bytes=(62 << 20) if heads else (66 << 20) - nbytes(panels)
        ),
        cost_estimate=pl.CostEstimate(
            flops=2 * count * halves * rows * depth * rep_count * row_count,
            bytes_accessed=2 * count * halves * rows * (depth + rep_count * row_count),
            transcendentals=0,
        ),
        name="partials",
    )(*tables, amp, panels, *extra)
    return results[:heads], results[heads:]


def gather_kernel(count_ids, factor, *refs):
    ids, parts = refs[:count_ids], refs[count_ids : 2 * count_ids]
    outs, ladders, own, sem = refs[-factor - 4 : -4], refs[-4:-2], refs[-2], refs[-1]
    count = own.shape[0]
    rest, tiles = outs[0].shape[:2]
    load = pltpu.make_async_copy(parts[0], own, sem)
    load.start()
    for ladder in ladders:
        ladder[...] = jnp.zeros_like(ladder)

    def add(left, right):
        for s in range(count):
            rows = []
            for ladder, (index, part) in zip(ladders, (left, right)):
                place = index[0, s]
                rows.append((ladder, place, ladder[place] + part[s].astype(jnp.float32)))
            for ladder, place, value in rows:
                ladder[place] = value

    received = list(zip(ids[1:], parts[1:]))
    add(received[0], received[1])
    load.wait()
    add(received[2], (ids[0], own))
    digit = lax.axis_index("blk") % factor
    for k in range(factor):
        for z in range(rest):
            span = pl.ds((z * factor + (digit ^ k)) * tiles, tiles)
            outs[k][z] = (ladders[0][span] + ladders[1][span]).astype(outs[k].dtype)


def gather_tiles(ids, parts, blk_count, tiles, factor, after=None):
    _, rows, _ = parts[0].shape
    shape = (blk_count // factor, tiles, rows, LANES)
    outs = [jax.ShapeDtypeStruct(shape, jnp.bfloat16 if k else jnp.float32) for k in range(factor)]
    ladder = pltpu.VMEM((blk_count * tiles, rows, LANES), jnp.float32)
    extra = [] if after is None else [after]
    return pl.pallas_call(
        functools.partial(gather_kernel, len(ids), factor),
        out_shape=outs,
        in_specs=[whole(pltpu.SMEM)] * len(ids)
        + [whole(pl.ANY)]
        + [whole()] * (len(parts) - 1)
        + [whole(pl.ANY)] * len(extra),
        out_specs=[whole()] * factor,
        scratch_shapes=[ladder] * 2
        + [pltpu.VMEM(parts[0].shape, parts[0].dtype), pltpu.SemaphoreType.DMA],
        compiler_params=grant(*parts, *outs, ladder, ladder),
        cost_estimate=pl.CostEstimate(
            flops=blk_count * tiles * rows * LANES,
            bytes_accessed=8 * blk_count * tiles * rows * LANES,
            transcendentals=0,
        ),
        name="gather_tiles",
    )(*ids, *parts, *extra)


def merge_kernel(arrays, factor, stride, *refs):
    ins, outs = refs[:arrays], refs[-factor:]
    rest = outs[0].shape[0]
    digit = (lax.axis_index("blk") // stride) % factor
    for k in range(factor):
        for z in range(rest):
            owner = z * factor + (digit ^ k)
            total = ins[0][owner]
            for other in ins[1:]:
                total = total + other[owner].astype(jnp.float32)
            outs[k][z] = total.astype(outs[k].dtype)


def merge(arrays, factor, stride, after=None):
    owners, tiles, rows, _ = arrays[0].shape
    shape = (owners // factor, tiles, rows, LANES)
    outs = [jax.ShapeDtypeStruct(shape, jnp.bfloat16 if k else jnp.float32) for k in range(factor)]
    extra = [] if after is None else [after]
    return pl.pallas_call(
        functools.partial(merge_kernel, len(arrays), factor, stride),
        out_shape=outs,
        in_specs=[whole()] * len(arrays) + [whole(pl.ANY)] * len(extra),
        out_specs=[whole()] * factor,
        compiler_params=grant(*arrays, *outs),
        cost_estimate=pl.CostEstimate(
            flops=owners * tiles * rows * LANES,
            bytes_accessed=8 * owners * tiles * rows * LANES,
            transcendentals=0,
        ),
        name="merge",
    )(*arrays, *extra)


def finish_kernel(per_part, *refs):
    occ, vir, keep, out = refs[0], refs[1], refs[2], refs[-1]
    ins = refs[3:-1]
    tiles = ins[0].shape[0]
    totals = []
    for start in range(0, len(ins), per_part):
        total = ins[start][...]
        for other in ins[start + 1 : start + per_part]:
            total = total + other[...].astype(jnp.float32)
        totals.append(total)
    total = jnp.concatenate(totals, axis=1)
    half = tiles // 2
    first, second = half_rows(total[:half], total[half:])
    rows = jnp.stack([first, second], axis=1).reshape(-1, LANES)
    flipped = rows.T
    columns = rows.shape[0]
    row_count = out.shape[0]
    for side in range(2):
        lanes = slice(side * columns, (side + 1) * columns)
        value = flipped[side * row_count : (side + 1) * row_count]
        denominator = occ[...] - vir[:, lanes]
        kept = keep[:, lanes] != 0
        out[:, lanes] = jnp.where(kept, value / denominator, 0.0).astype(jnp.bfloat16)


def finish(occ, vir, keep, arrays, per_part):
    out = jax.ShapeDtypeStruct((occ.shape[0], vir.shape[1]), jnp.bfloat16)
    return pl.pallas_call(
        functools.partial(finish_kernel, per_part),
        out_shape=out,
        in_specs=[whole()] * (3 + len(arrays)),
        out_specs=whole(),
        compiler_params=grant(out, out, out, *arrays),
        name="finish",
    )(occ, vir, keep, *arrays)


def shards(
    amplitudes,
    panels,
    panel_owner_index,
    panel_target_tile,
    panel_tile_mask,
    tile_sizes,
    tile_irreps,
    occ_energy,
    vir_energy,
):
    blk_count = lax.axis_size("blk")
    rep_count = lax.axis_size("rep")
    blk_index = lax.axis_index("blk")
    count, width, depth = panels.shape
    tiles_here = depth // width
    owned = tiles_here * rep_count
    row_count = amplitudes.shape[0] // rep_count
    halves = LANES // row_count
    packed = width // halves
    factors = stage_factors(blk_count)

    amp = amplitudes.reshape(rep_count, row_count, depth)
    panels = panels.reshape(count, halves, packed, depth)
    tables = [
        panel_owner_index.T,
        panel_target_tile,
        panel_tile_mask.T,
        tile_sizes,
        tile_irreps,
    ]

    def swap_rep(value, k):
        return lax.ppermute(value, "rep", [(i, i ^ k) for i in range(rep_count)])

    def swap_blk(value, k):
        return lax.ppermute(value, "blk", [(i, i ^ k) for i in range(blk_count)])

    spans, first = [], 0
    for share in SHARES:
        rows = packed * share // sum(SHARES)
        spans.append((first, rows))
        first += rows

    last, ids, strides = None, None, [1]
    for factor in factors:
        strides.append(strides[-1] * factor)
    pending = [None] * len(spans)
    for part, stage in task_order(len(spans), len(factors)):
        if stage < 0:
            heads, (own, *others) = partials(tables, amp, panels, spans[part], owned, last)
            last = own
        elif stage == 0:
            arrays = gather_tiles(ids, pending[part], blk_count, owned, factors[0], last)
            last = arrays[0]
        else:
            arrays = merge(pending[part], factors[stage], strides[stage], last)
            last = arrays[0]
        if stage < 0:
            swapped = [swap_rep(others[k - 1], k) for k in range(1, rep_count)]
            pending[part] = [own, *swapped]
            if heads:
                tables = heads[1:]
                ids = [heads[0]] + [swap_rep(heads[0], k) for k in range(1, rep_count)]
        else:
            stride = strides[stage]
            swapped = [swap_blk(arrays[k], k * stride) for k in range(1, factors[stage])]
            pending[part] = [arrays[0], *swapped]
    collected = [value[0] for part in pending for value in part]

    sizes_owned = lax.dynamic_slice_in_dim(tile_sizes, blk_index * owned, owned, 0)
    in_tile = jnp.arange(width, dtype=jnp.int32)
    keep = (in_tile[None, :] < sizes_owned[:, None]).astype(jnp.int32).reshape(1, owned * width)
    return finish(
        occ_energy[:, None], vir_energy[None, :], keep, collected, len(pending[0])
    )


def solution(mesh):
    return jax.shard_map(
        shards,
        mesh=mesh,
        in_specs=(
            P(None, ("blk", "rep")),
            P(("blk", "rep"), None, None),
            P(("blk", "rep"), None),
            P(("blk", "rep")),
            P(("blk", "rep"), None),
            P(),
            P(),
            P("rep"),
            P("blk"),
        ),
        out_specs=P("rep", "blk"),
        check_vma=False,
    )
```

```python
import functools

import jax
import jax.numpy as jnp
from jax import lax
from jax.experimental import pallas as pl
from jax.experimental.pallas import tpu as pltpu
from jax.sharding import PartitionSpec as P

LANES = 128
COPY_PANELS = 43
SHARES = (4, 3, 3, 2)
MAKES = ((1, -3), (1, -2), (1, -1), (1, 0.4))


def stage_factors(count):
    factors, rest = [], count
    while rest > 1:
        factor = min(4 if factors else 2, rest)
        factors.append(factor)
        rest //= factor
    return factors


def task_order(parts, stages):
    keys, start = [], 0
    for size, when in MAKES:
        keys.append((when, range(start, min(start + size, parts)), -1))
        start += size
    keys += [
        (part + 1.5 * stage, range(part, part + 1), stage)
        for part in range(parts)
        for stage in range(stages)
    ]
    return [(group, stage) for _, group, stage in sorted(keys, key=lambda item: item[0])]


def whole(memory_space=pltpu.VMEM):
    return pl.BlockSpec(memory_space=memory_space)


def nbytes(*arrays):
    total = 0
    for a in arrays:
        size = jnp.dtype(a.dtype).itemsize
        for d in a.shape:
            size *= d
        total += size
    return total


def grant(*arrays):
    return pltpu.CompilerParams(vmem_limit_bytes=min(62 << 20, nbytes(*arrays) * 3 // 2 + (4 << 20)))


def half_rows(low, high):
    lane = lax.broadcasted_iota(jnp.int32, low.shape, low.ndim - 1)
    width = LANES // 2
    first = jnp.where(lane < width, low, pltpu.roll(high, width, high.ndim - 1))
    second = jnp.where(lane < width, pltpu.roll(low, width, low.ndim - 1), high)
    return first, second


def column_sum(pick, values):
    return jnp.sum(jnp.where(pick, values, 0.0), axis=1, keepdims=True)


def live_factors(owner, tile, mask, sizes, irreps, device, owned, depth):
    tiles, count = mask.shape
    width, total = depth // tiles, sizes.shape[-1]
    eye = lax.broadcasted_iota(jnp.int32, (count, count), 0) == lax.broadcasted_iota(
        jnp.int32, (count, count), 1
    )
    size_row = sizes.reshape(1, total).astype(jnp.float32)
    irrep_row = irreps.reshape(1, total).astype(jnp.float32)
    target_row = owner * owned + tile.reshape(1, count)
    target = column_sum(eye, target_row.astype(jnp.float32)).astype(jnp.int32)
    tile_index = lax.broadcasted_iota(jnp.int32, (count, total), 1)
    irrep_target = column_sum(tile_index == target, irrep_row)
    column = lax.broadcasted_iota(jnp.int32, (count, depth), 1)
    keep = None
    for j in range(tiles):
        source = tile_index[:1] == device * tiles + j
        masked = column_sum(eye, mask[j : j + 1, :].astype(jnp.float32))
        live = (masked != 0.0) & (irrep_target == column_sum(source, irrep_row))
        limit = jnp.where(live, column_sum(source, size_row), 0.0).astype(jnp.int32)
        inside = (column >= j * width) & (column < j * width + limit)
        keep = inside if keep is None else keep | inside
    return target_row, keep.astype(jnp.float32)


def partial_kernel(spans, owned, tables, *refs):
    amp, panels = refs[tables : tables + 2]
    outs, (amp_here, sem, small) = refs[tables + 2 : -3], refs[-3:]
    buffers = outs[-len(spans) :]
    copied = outs[-len(spans) - tables : -len(spans)]
    rep_count, row_count, depth = amp.shape
    count = panels.shape[0]
    loads = [
        pltpu.make_async_copy(source, target, small.at[i])
        for i, (source, target) in enumerate(zip((*refs[:tables], amp), (*copied, amp_here)))
    ]
    for load in loads:
        load.start()
    copies = []
    for (first, rows), buffer in zip(spans, buffers):
        for start in range(0, count, COPY_PANELS):
            piece = pl.ds(start, min(COPY_PANELS, count - start))
            copies.append(
                pltpu.make_async_copy(
                    panels.at[piece, :, pl.ds(first, rows)],
                    buffer.at[piece],
                    sem.at[len(copies)],
                )
            )
            copies[-1].start()
    for load in loads:
        load.wait()

    rep_index = lax.axis_index("rep")
    amp_t = jnp.concatenate([amp_here[rep_index ^ k] for k in range(rep_count)], axis=0).T
    if tables > 1:
        device = lax.axis_index("blk") * rep_count + rep_index
        ids, factors, *outs = outs
        ids[...], factors[...] = live_factors(*[t[...] for t in copied], device, owned, depth)
    else:
        factors = copied[0]

    factor = factors[...].astype(jnp.bfloat16)
    pieces = len(copies) // len(spans)
    for part, ((_, rows), buffer) in enumerate(zip(spans, buffers)):
        for copy in copies[part * pieces : (part + 1) * pieces]:
            copy.wait()
        halves = buffer.shape[1]
        live_panels = buffer[...] * factor[:, None, None, :]
        product = jnp.dot(
            live_panels.reshape(count * halves * rows, depth),
            amp_t,
            preferred_element_type=jnp.float32,
        )
        product = product.reshape(count, halves, rows, rep_count * row_count)
        for pair in range(rep_count // 2):
            lanes = slice(pair * LANES, (pair + 1) * LANES)
            packed = half_rows(product[:, 0, :, lanes], product[:, 1, :, lanes])
            for side, value in enumerate(packed):
                outs[part * rep_count + 2 * pair + side][...] = value.astype(jnp.bfloat16)


def partials(tables, amp, panels, spans, owned):
    count, halves, _, depth = panels.shape
    rep_count, row_count, _ = amp.shape
    total = sum(rows for _, rows in spans)
    outs = []
    if len(tables) > 1:
        outs += [
            jax.ShapeDtypeStruct((1, count), jnp.int32),
            jax.ShapeDtypeStruct((count, depth), jnp.float32),
        ]
    heads = len(outs)
    for _, rows in spans:
        outs += [jax.ShapeDtypeStruct((count, rows, LANES), jnp.bfloat16)] * rep_count
    results = pl.pallas_call(
        functools.partial(partial_kernel, spans, owned, len(tables)),
        out_shape=outs,
        in_specs=[whole(pl.ANY)] * (len(tables) + 2),
        out_specs=[whole()] * len(outs),
        scratch_shapes=[
            *[pltpu.VMEM(t.shape, t.dtype) for t in tables],
            *[pltpu.VMEM((count, halves, rows, depth), jnp.bfloat16) for _, rows in spans],
            pltpu.VMEM(amp.shape, amp.dtype),
            pltpu.SemaphoreType.DMA((pl.cdiv(count, COPY_PANELS) * len(spans),)),
            pltpu.SemaphoreType.DMA((len(tables) + 1,)),
        ],
        compiler_params=pltpu.CompilerParams(
            vmem_limit_bytes=(62 << 20) if heads else (66 << 20) - nbytes(panels)
        ),
        cost_estimate=pl.CostEstimate(
            flops=2 * count * halves * total * depth * rep_count * row_count,
            bytes_accessed=2 * count * halves * total * (depth + rep_count * row_count),
            transcendentals=0,
        ),
        name="partials",
    )(*tables, amp, panels)
    parts = results[heads:]
    return results[:heads], [
        parts[i * rep_count : (i + 1) * rep_count] for i in range(len(spans))
    ]


def gather_kernel(count_ids, factor, *refs):
    ids, parts = refs[:count_ids], refs[count_ids : 2 * count_ids]
    outs, ladders, own, sem = refs[-factor - 4 : -4], refs[-4:-2], refs[-2], refs[-1]
    count = own.shape[0]
    rest, tiles = outs[0].shape[:2]
    load = pltpu.make_async_copy(parts[0], own, sem)
    load.start()
    for ladder in ladders:
        ladder[...] = jnp.zeros_like(ladder)

    def add(left, right):
        for s in range(count):
            rows = []
            for ladder, (index, part) in zip(ladders, (left, right)):
                place = index[0, s]
                rows.append((ladder, place, ladder[place] + part[s].astype(jnp.float32)))
            for ladder, place, value in rows:
                ladder[place] = value

    received = list(zip(ids[1:], parts[1:]))
    add(received[0], received[1])
    load.wait()
    add(received[2], (ids[0], own))
    digit = lax.axis_index("blk") % factor
    for k in range(factor):
        for z in range(rest):
            span = pl.ds((z * factor + (digit ^ k)) * tiles, tiles)
            outs[k][z] = (ladders[0][span] + ladders[1][span]).astype(outs[k].dtype)


def gather_tiles(ids, parts, blk_count, tiles, factor):
    _, rows, _ = parts[0].shape
    shape = (blk_count // factor, tiles, rows, LANES)
    outs = [jax.ShapeDtypeStruct(shape, jnp.bfloat16 if k else jnp.float32) for k in range(factor)]
    ladder = pltpu.VMEM((blk_count * tiles, rows, LANES), jnp.float32)
    return pl.pallas_call(
        functools.partial(gather_kernel, len(ids), factor),
        out_shape=outs,
        in_specs=[whole(pltpu.SMEM)] * len(ids)
        + [whole(pl.ANY)]
        + [whole()] * (len(parts) - 1),
        out_specs=[whole()] * factor,
        scratch_shapes=[ladder] * 2
        + [pltpu.VMEM(parts[0].shape, parts[0].dtype), pltpu.SemaphoreType.DMA],
        compiler_params=grant(*parts, *outs, ladder, ladder),
        cost_estimate=pl.CostEstimate(
            flops=blk_count * tiles * rows * LANES,
            bytes_accessed=8 * blk_count * tiles * rows * LANES,
            transcendentals=0,
        ),
        name="gather_tiles",
    )(*ids, *parts)


def merge_kernel(arrays, factor, stride, *refs):
    ins, outs = refs[:arrays], refs[-factor:]
    rest = outs[0].shape[0]
    digit = (lax.axis_index("blk") // stride) % factor
    for k in range(factor):
        for z in range(rest):
            owner = z * factor + (digit ^ k)
            total = ins[0][owner]
            for other in ins[1:]:
                total = total + other[owner].astype(jnp.float32)
            outs[k][z] = total.astype(outs[k].dtype)


def merge(arrays, factor, stride):
    owners, tiles, rows, _ = arrays[0].shape
    shape = (owners // factor, tiles, rows, LANES)
    outs = [jax.ShapeDtypeStruct(shape, jnp.bfloat16 if k else jnp.float32) for k in range(factor)]
    return pl.pallas_call(
        functools.partial(merge_kernel, len(arrays), factor, stride),
        out_shape=outs,
        in_specs=[whole()] * len(arrays),
        out_specs=[whole()] * factor,
        compiler_params=grant(*arrays, *outs),
        cost_estimate=pl.CostEstimate(
            flops=owners * tiles * rows * LANES,
            bytes_accessed=8 * owners * tiles * rows * LANES,
            transcendentals=0,
        ),
        name="merge",
    )(*arrays)


def finish_kernel(per_part, *refs):
    occ, vir, keep, out = refs[0], refs[1], refs[2], refs[-1]
    ins = refs[3:-1]
    tiles = ins[0].shape[0]
    totals = []
    for start in range(0, len(ins), per_part):
        total = ins[start][...]
        for other in ins[start + 1 : start + per_part]:
            total = total + other[...].astype(jnp.float32)
        totals.append(total)
    total = jnp.concatenate(totals, axis=1)
    half = tiles // 2
    first, second = half_rows(total[:half], total[half:])
    rows = jnp.stack([first, second], axis=1).reshape(-1, LANES)
    flipped = rows.T
    columns = rows.shape[0]
    row_count = out.shape[0]
    for side in range(2):
        lanes = slice(side * columns, (side + 1) * columns)
        value = flipped[side * row_count : (side + 1) * row_count]
        denominator = occ[...] - vir[:, lanes]
        kept = keep[:, lanes] != 0
        out[:, lanes] = jnp.where(kept, value / denominator, 0.0).astype(jnp.bfloat16)


def finish(occ, vir, keep, arrays, per_part):
    out = jax.ShapeDtypeStruct((occ.shape[0], vir.shape[1]), jnp.bfloat16)
    return pl.pallas_call(
        functools.partial(finish_kernel, per_part),
        out_shape=out,
        in_specs=[whole()] * (3 + len(arrays)),
        out_specs=whole(),
        compiler_params=grant(out, out, out, *arrays),
        name="finish",
    )(occ, vir, keep, *arrays)


def shards(
    amplitudes,
    panels,
    panel_owner_index,
    panel_target_tile,
    panel_tile_mask,
    tile_sizes,
    tile_irreps,
    occ_energy,
    vir_energy,
):
    blk_count = lax.axis_size("blk")
    rep_count = lax.axis_size("rep")
    blk_index = lax.axis_index("blk")
    count, width, depth = panels.shape
    tiles_here = depth // width
    owned = tiles_here * rep_count
    row_count = amplitudes.shape[0] // rep_count
    halves = LANES // row_count
    packed = width // halves
    factors = stage_factors(blk_count)

    amp = amplitudes.reshape(rep_count, row_count, depth)
    panels = panels.reshape(count, halves, packed, depth)
    tables = [
        panel_owner_index.T,
        panel_target_tile,
        panel_tile_mask.T,
        tile_sizes,
        tile_irreps,
    ]

    def swap_rep(value, k):
        return lax.ppermute(value, "rep", [(i, i ^ k) for i in range(rep_count)])

    def swap_blk(value, k):
        return lax.ppermute(value, "blk", [(i, i ^ k) for i in range(blk_count)])

    spans, first = [], 0
    for share in SHARES:
        rows = packed * share // sum(SHARES)
        spans.append((first, rows))
        first += rows

    ids, strides = None, [1]
    for factor in factors:
        strides.append(strides[-1] * factor)
    pending = [None] * len(spans)
    for group, stage in task_order(len(spans), len(factors)):
        if stage < 0:
            group_spans = [spans[part] for part in group]
            heads, made = partials(tables, amp, panels, group_spans, owned)
        elif stage == 0:
            part = group[0]
            arrays = gather_tiles(ids, pending[part], blk_count, owned, factors[0])
        else:
            part = group[0]
            arrays = merge(pending[part], factors[stage], strides[stage])
        if stage < 0:
            for part, (own, *others) in zip(group, made):
                swapped = [swap_rep(others[k - 1], k) for k in range(1, rep_count)]
                pending[part] = [own, *swapped]
            if heads:
                tables = heads[1:]
                ids = [heads[0]] + [swap_rep(heads[0], k) for k in range(1, rep_count)]
        else:
            stride, peers = strides[stage], factors[stage]
            swapped = [swap_blk(arrays[k], k * stride) for k in range(1, peers)]
            pending[part] = [arrays[0], *swapped]
    collected = [value[0] for part in pending for value in part]

    sizes_owned = lax.dynamic_slice_in_dim(tile_sizes, blk_index * owned, owned, 0)
    in_tile = jnp.arange(width, dtype=jnp.int32)
    keep = (in_tile[None, :] < sizes_owned[:, None]).astype(jnp.int32).reshape(1, owned * width)
    return finish(
        occ_energy[:, None], vir_energy[None, :], keep, collected, len(pending[0])
    )


def solution(mesh):
    return jax.shard_map(
        shards,
        mesh=mesh,
        in_specs=(
            P(None, ("blk", "rep")),
            P(("blk", "rep"), None, None),
            P(("blk", "rep"), None),
            P(("blk", "rep")),
            P(("blk", "rep"), None),
            P(),
            P(),
            P("rep"),
            P("blk"),
        ),
        out_specs=P("rep", "blk"),
        check_vma=False,
    )
```
